32 devices in a mesh: pipe: 2 (over core), dp: 16 (over z, y, x).
Axes of the slice: x: 2, y: 2, z: 4, core: 2. Of those that a mesh axis runs over, the one named last changes fastest.
Arguments:
- feats: bfloat16 [256, 8, 10, 768], P('dp'), may hold values from -6 to 6
- dw_kernel: bfloat16 [2, 7, 7, 768], P('pipe'), may hold values from -0.875 to 0.875
- ln_gain: float32 [2, 768], P('pipe'), may hold values from 0.25 to 1.75
- w_in: bfloat16 [2, 768, 3072], P('pipe'), may hold values from -0.21875 to 0.21875
- w_out: bfloat16 [2, 3072, 768], P('pipe'), may hold values from -0.109375 to 0.109375
- layer_scale: float32 [2, 768], P('pipe'), may hold values from 0.3 to 3
- head_gain: float32 [768], replicated, may hold values from 0.25 to 1.75
- head_proj: bfloat16 [768, 1024], replicated, may hold values from -0.21875 to 0.21875
- yield_embeds: bfloat16 [2048, 1024], P(('pipe', 'dp')), may hold values from -0.19921875 to 0.19921875
- match_ids: int32 [256], P('dp'), may hold values from 0 to 2047
- logit_scale: float32 [], replicated, may hold values from 5 to 20
- logit_bias: float32 [], replicated, may hold values from -4 to -1
Outputs:
- projected: bfloat16 [256, 1024], P('dp')
- embed_grad: float32 [256, 1024], P('dp')
The draws below stay inside these ranges and needn't reach their ends.
Inputs may be any that keep to these rules, and one draw needn't show every extreme that they name: `match_ids`: index of the yield embedding paired with each image.
All inputs are finite; a program needn't handle non-finite values.
Results may differ from the reference program's by a relative error of at most 0.015.
Values may be sent and summed in bfloat16 or wider, within the bound.
A program may use at most 128 MiB of HBM per device.

```python
import math
import jax
import jax.numpy as jnp
from jax import lax

C = 768
HID = 3072
E = 1024
KS = 7
HH = 8
WW = 10
SECT = 2
IMAGES = 256
YIELDS = 2048


def plant(array, key, least, largest):
    shape = array.shape
    index_at = [jax.random.randint(jax.random.fold_in(key, axis), (), 0, shape[axis]) for axis in range(len(shape))]
    array = array.at[tuple(index_at)].set(least)
    longest = shape.index(max(shape))
    index_at[longest] = (index_at[longest] + 1) % shape[longest]
    return array.at[tuple(index_at)].set(largest)


def levels(stream_key, dims, pieces, least, high):
    loudness = 1.0
    for position, blocks in pieces:
        heights = jax.random.uniform(jax.random.fold_in(jax.random.fold_in(stream_key, 6), position), (blocks,), jnp.float32, least / len(pieces), high / len(pieces))
        loudness = loudness * jnp.repeat(jnp.exp(heights), dims[position] // blocks).reshape((-1,) + (1,) * (len(dims) - 1 - position))
    return loudness


def gaussian(key, shape, scale, most, cuts=(), held_as=jnp.bfloat16):
    factor_of = levels(key, shape, cuts, -0.22, 0.18) if cuts else 1.0
    values = jax.random.normal(key, shape, jnp.float32) * scale * factor_of
    return jnp.minimum(jnp.maximum(values, -most), most).astype(held_as)


def setup_inputs(seed: int = 0) -> dict:
    splits = jax.random.split(jax.random.key(seed), 13)
    feats = gaussian(splits[0], (IMAGES, HH, WW, C), 1.0, 6.0, ((0, 16),))
    dw_kernel = gaussian(splits[1], (SECT, KS, KS, C), (KS * KS) ** -0.5, 0.875, ((0, 2),))
    ln_gain = jnp.clip(1.0 + 0.15 * jax.random.normal(splits[2], (SECT, C), jnp.float32), 0.25, 1.75)
    w_in = gaussian(splits[3], (SECT, C, HID), C ** -0.5, 0.21875, ((0, 2),))
    w_out = gaussian(splits[4], (SECT, HID, C), HID ** -0.5, 0.109375, ((0, 2),))
    layer_scale = jnp.clip(jnp.exp(math.log(3.0) - 2.3025851 * jax.random.uniform(splits[5], (SECT, C), jnp.float32) ** levels(splits[5], (SECT, C), ((0, 2),), -0.2, 0.2)), 0.3, 3.0)
    head_gain = jnp.clip(1.0 + 0.15 * jax.random.normal(splits[6], (C,), jnp.float32), 0.25, 1.75)
    head_proj = gaussian(splits[7], (C, E), C ** -0.5, 0.21875)
    yield_embeds = gaussian(splits[8], (YIELDS, E), 0.03125, 0.19921875, ((0, 32),))
    match_ids = plant(jax.random.randint(splits[9], (IMAGES,), 0, YIELDS), jax.random.fold_in(splits[9], 1), 0, YIELDS - 1).astype(jnp.int32)
    logit_scale = jnp.clip(jnp.exp(jax.random.uniform(splits[10], (), jnp.float32, math.log(5.0), math.log(20.0))), 5.0, 20.0)
    logit_bias = jnp.clip(jax.random.uniform(splits[11], (), jnp.float32, -4.0, -1.0), -4.0, -1.0)
    return {"feats": feats, "dw_kernel": dw_kernel, "ln_gain": ln_gain, "w_in": w_in, "w_out": w_out, "layer_scale": layer_scale, "head_gain": head_gain, "head_proj": head_proj, "yield_embeds": yield_embeds, "match_ids": match_ids, "logit_scale": logit_scale, "logit_bias": logit_bias}


def layer_norm(value, gain):
    mean = lax.optimization_barrier(jnp.mean(value, axis=-1, keepdims=True))
    centred = value - mean
    var = lax.optimization_barrier(jnp.mean(centred * centred, axis=-1, keepdims=True))
    return centred * lax.rsqrt(var + 1e-06) * gain

def depthwise(act, kernel):
    rows = act.shape[0]
    cols = act.shape[1]
    padded = jnp.pad(act.astype(jnp.float32), ((3, 3), (3, 3), (0, 0)))
    kernel32 = kernel.astype(jnp.float32)
    total = jnp.zeros(act.shape, jnp.float32)
    for row_off in range(7):
        for col_off in range(7):
            total = total + padded[row_off:row_off + rows, col_off:col_off + cols, :] * kernel32[row_off, col_off]
    return total

def block(act, kernel, gain, weight_in, weight_out, scale):
    channels = act.shape[-1]
    conv = depthwise(act, kernel)
    normed = layer_norm(conv, gain).astype(jnp.bfloat16).reshape(-1, channels)
    hidden = jax.nn.gelu(jnp.dot(normed, weight_in, preferred_element_type=jnp.float32), approximate=False).astype(jnp.bfloat16)
    branch = jnp.dot(hidden, weight_out, preferred_element_type=jnp.float32)
    result = act.reshape(-1, channels).astype(jnp.float32) + scale * branch
    return result.astype(jnp.bfloat16).reshape(act.shape)

def section_fn(dw_kernel, ln_gain, w_in, w_out, layer_scale, index):

    def apply(act):
        return block(act, dw_kernel[index], ln_gain[index], w_in[index], w_out[index], layer_scale[index])
    return apply

def reference(feats, dw_kernel, ln_gain, w_in, w_out, layer_scale, head_gain, head_proj, yield_embeds, match_ids, logit_scale, logit_bias):
    act = feats
    for index in range(SECT):
        act = lax.map(section_fn(dw_kernel, ln_gain, w_in, w_out, layer_scale, index), act)
    pooled = lax.optimization_barrier(jnp.mean(act.astype(jnp.float32), axis=(1, 2)))
    head_normed = layer_norm(pooled, head_gain).astype(jnp.bfloat16)
    projected = jnp.dot(head_normed, head_proj, preferred_element_type=jnp.float32).astype(jnp.bfloat16)
    wide = projected.astype(jnp.float32)
    unit = (wide / jnp.sqrt(lax.optimization_barrier(jnp.sum(wide * wide, axis=-1, keepdims=True)) + 1e-06)).astype(jnp.bfloat16)
    logits = logit_scale * jnp.dot(unit, yield_embeds.T, preferred_element_type=jnp.float32) + logit_bias
    columns = jnp.arange(YIELDS, dtype=jnp.int32)
    label = jnp.where(match_ids[:, None] == columns[None, :], 1.0, -1.0).astype(jnp.float32)
    coef = (-label * logit_scale * jax.nn.sigmoid(-label * logits)).astype(jnp.bfloat16)
    embed_grad = jnp.dot(coef, yield_embeds, preferred_element_type=jnp.float32)
    return (projected, embed_grad)
```

```python
import functools

import jax
import jax.numpy as jnp
from jax import lax
from jax.experimental import pallas as pl
from jax.experimental.pallas import tpu as pltpu
from jax.sharding import PartitionSpec as P

CHUNK = 256
LANES = 128
ERF_POLY = (
    7.97872669e-01,
    3.63655561e-02,
    -5.77947342e-05,
    -4.72814832e-05,
    2.79985521e-06,
    -5.66473023e-08,
)
ERF_EDGE = 5.5 * 5.5


def gelu(x):
    x2 = jnp.minimum(x * x, ERF_EDGE)
    poly = ERF_POLY[-1]
    for coefficient in ERF_POLY[-2::-1]:
        poly = poly * x2 + coefficient
    half = 0.5 * x
    return half + half * jnp.tanh(x * poly)


def normalise(value, gain):
    mean = jnp.mean(value, axis=-1, keepdims=True)
    centred = value - mean
    var = jnp.mean(centred * centred, axis=-1, keepdims=True)
    return centred * lax.rsqrt(var + 1e-06) * gain


def tower_kernel(
    taps,
    feats_hbm,
    small_hbm,
    win_hbm,
    wout_hbm,
    hgain_ref,
    hproj_ref,
    out_ref,
    feats,
    small,
    win,
    wout,
    act,
    conv,
    normed,
    acc,
    raw_a,
    raw_b,
    wide_taps,
    proj,
    feat_sem,
    small_sem,
    in_sem,
    out_sem,
    small_send,
    in_send,
    out_send,
    proj_send,
    proj_recv,
):
    images, rows, cols, channels = feats.shape
    sections = win.shape[0]
    chunks = win.shape[1]
    places = rows * cols
    reach = taps // 2
    me = lax.axis_index("pipe")
    other = 1 - me
    peer = {"pipe": other}

    def in_source(c):
        return win_hbm.at[:, pl.ds(pl.multiple_of(c * CHUNK, CHUNK), CHUNK)]

    def out_source(c):
        return wout_hbm.at[pl.ds(pl.multiple_of(c * CHUNK, CHUNK), CHUNK), :]

    def local_small():
        return pltpu.make_async_copy(small_hbm, small.at[me], small_sem.at[me])

    def local_in(c):
        return pltpu.make_async_copy(in_source(c), win.at[me, c], in_sem.at[me, c])

    def local_out(c):
        return pltpu.make_async_copy(out_source(c), wout.at[me, c], out_sem.at[me, c])

    def remote(source, target, send, recv):
        return pltpu.make_async_remote_copy(
            src_ref=source,
            dst_ref=target,
            send_sem=send,
            recv_sem=recv,
            device_id=peer,
            device_id_type=pl.DeviceIdType.MESH,
        )

    def remote_small(section):
        return remote(small_hbm, small.at[section], small_send, small_sem.at[section])

    def remote_in(section, c):
        return remote(in_source(c), win.at[section, c], in_send.at[c], in_sem.at[section, c])

    def remote_out(section, c):
        return remote(out_source(c), wout.at[section, c], out_send.at[c], out_sem.at[section, c])

    fetch = pltpu.make_async_copy(feats_hbm.at[pl.ds(me * images, images)], feats, feat_sem)
    fetch.start()
    local_small().start()

    barrier = pltpu.get_barrier_semaphore()
    pl.semaphore_signal(barrier, inc=1, device_id=peer, device_id_type=pl.DeviceIdType.MESH)
    pl.semaphore_wait(barrier, 1)

    remote_small(me).start()

    def begin(c, carry):
        remote_in(me, c).start()
        local_in(c).start()
        remote_out(me, c).start()
        local_out(c).start()
        return carry

    lax.fori_loop(0, chunks, begin, 0)

    def await_small(section):
        @pl.when(section == me)
        def _():
            local_small().wait()

        @pl.when(section != me)
        def _():
            remote_small(section).wait_recv()

    def await_chunk(section, c):
        @pl.when(section == me)
        def _():
            local_in(c).wait()
            local_out(c).wait()

        @pl.when(section != me)
        def _():
            remote_in(section, c).wait_recv()
            remote_out(section, c).wait_recv()

    fetch.wait()

    def spread(image, carry):
        for r in range(rows):
            line = feats[image, r].astype(jnp.float32)
            for block in range(channels // LANES):
                act[block, pl.ds(r * cols * images + image, cols, stride=images), :] = line[
                    :, block * LANES : (block + 1) * LANES
                ]
        return carry

    for image in range(images):
        spread(image, 0)

    def one_section(section, carry):
        await_small(section)

        def conv_lanes(block, inner):
            lanes = pl.ds(pl.multiple_of(block * LANES, LANES), LANES)
            for k in range(taps * taps):
                wide_taps[k] = jnp.broadcast_to(small[section, pl.ds(k, 1), lanes], (images, LANES))
            for r in range(rows):
                total = [None] * cols
                for dy in range(taps):
                    source = r + dy - reach
                    if not 0 <= source < rows:
                        continue
                    kernel = [wide_taps[dy * taps + dx] for dx in range(taps)]
                    line = [
                        act[block, pl.ds((source * cols + w) * images, images), :]
                        for w in range(cols)
                    ]
                    for w in range(cols):
                        for dx in range(taps):
                            at = w + dx - reach
                            if not 0 <= at < cols:
                                continue
                            term = line[at] * kernel[dx]
                            total[w] = term if total[w] is None else total[w] + term
                for w in range(cols):
                    conv[pl.ds((r * cols + w) * images, images), lanes] = total[w]
            return inner

        lax.fori_loop(0, channels // LANES, conv_lanes, 0)

        gain = small[section, pl.ds(taps * taps, 1), :]
        step_rows = 32

        def norm_rows(block, inner):
            at = pl.ds(pl.multiple_of(block * step_rows, step_rows), step_rows)
            normed[at, :] = normalise(conv[at, :], gain).astype(jnp.bfloat16)
            return inner

        lax.fori_loop(0, places * images // step_rows, norm_rows, 0, unroll=4)

        acc[...] = jnp.zeros_like(acc)
        await_chunk(section, 0)
        raw_a[...] = jnp.dot(normed[...], win[section, 0], preferred_element_type=jnp.float32)

        def pair(j, inner):
            first = 2 * j
            after = jnp.minimum(first + 2, chunks - 1)
            await_chunk(section, first + 1)

            @pl.when(first + 2 < chunks)
            def _():
                await_chunk(section, after)

            raw_b[...] = jnp.dot(
                normed[...], win[section, first + 1], preferred_element_type=jnp.float32
            )
            acc[...] += jnp.dot(
                gelu(raw_a[...]).astype(jnp.bfloat16),
                wout[section, first],
                preferred_element_type=jnp.float32,
            )
            raw_a[...] = jnp.dot(
                normed[...], win[section, after], preferred_element_type=jnp.float32
            )
            acc[...] += jnp.dot(
                gelu(raw_b[...]).astype(jnp.bfloat16),
                wout[section, first + 1],
                preferred_element_type=jnp.float32,
            )
            return inner

        lax.fori_loop(0, chunks // 2, pair, 0)

        scale = small[section, pl.ds(taps * taps + 1, 1), :]

        def add_rows(block, inner):
            at = pl.ds(pl.multiple_of(block * step_rows, step_rows), step_rows)
            for lane in range(channels // LANES):
                lanes = slice(lane * LANES, (lane + 1) * LANES)
                total = act[lane, at, :] + scale[:, lanes] * acc[at, lanes]
                act[lane, at, :] = total.astype(jnp.bfloat16).astype(jnp.float32)
            return inner

        lax.fori_loop(0, places * images // step_rows, add_rows, 0, unroll=4)
        return carry

    lax.fori_loop(0, sections, one_section, 0)

    def pool(place, total):
        at = pl.ds(pl.multiple_of(place * images, images), images)
        return tuple(part + act[lane, at, :] for lane, part in enumerate(total))

    start = (jnp.zeros((images, LANES), jnp.float32),) * (channels // LANES)
    pooled = lax.fori_loop(0, places, pool, start, unroll=8)
    pooled = jnp.concatenate(pooled, axis=1) * (1.0 / places)
    head = normalise(pooled, hgain_ref[...]).astype(jnp.bfloat16)
    proj[me] = jnp.dot(head, hproj_ref[...], preferred_element_type=jnp.float32).astype(
        jnp.bfloat16
    )
    swap = remote(proj.at[me], proj.at[me], proj_send, proj_recv)
    swap.start()

    def finish(c, carry):
        remote_in(me, c).wait_send()
        remote_out(me, c).wait_send()
        return carry

    remote_small(me).wait_send()
    lax.fori_loop(0, chunks, finish, 0)
    swap.wait_send()
    remote(proj.at[other], proj.at[other], proj_send, proj_recv).wait_recv()
    out_ref[...] = proj[...]


def tower(feats, small, w_in, w_out, head_gain, head_proj, taps):
    sections = lax.axis_size("pipe")
    images = feats.shape[0] // sections
    rows, cols, channels = feats.shape[1:]
    hidden = w_in.shape[1]
    width = head_proj.shape[1]
    chunks = hidden // CHUNK
    cells = rows * cols * images
    f32, b16 = jnp.float32, jnp.bfloat16
    dma = pltpu.SemaphoreType.DMA
    anywhere = pl.BlockSpec(memory_space=pl.ANY)
    vmem = pl.BlockSpec(memory_space=pltpu.VMEM)
    return pl.pallas_call(
        functools.partial(tower_kernel, taps),
        out_shape=jax.ShapeDtypeStruct((sections, images, width), b16),
        in_specs=[anywhere, anywhere, anywhere, anywhere, vmem, vmem],
        out_specs=vmem,
        scratch_shapes=[
            pltpu.VMEM((images, rows, cols, channels), b16),
            pltpu.VMEM((sections,) + small.shape, f32),
            pltpu.VMEM((sections, chunks, channels, CHUNK), b16),
            pltpu.VMEM((sections, chunks, CHUNK, channels), b16),
            pltpu.VMEM((channels // LANES, cells, LANES), f32),
            pltpu.VMEM((cells, channels), f32),
            pltpu.VMEM((cells, channels), b16),
            pltpu.VMEM((cells, channels), f32),
            pltpu.VMEM((cells, CHUNK), f32),
            pltpu.VMEM((cells, CHUNK), f32),
            pltpu.VMEM((taps * taps, images, LANES), f32),
            pltpu.VMEM((sections, images, width), b16),
            dma,
            dma((sections,)),
            dma((sections, chunks)),
            dma((sections, chunks)),
            dma,
            dma((chunks,)),
            dma((chunks,)),
            dma,
            dma,
        ],
        compiler_params=pltpu.CompilerParams(
            collective_id=0, has_side_effects=True, vmem_limit_bytes=52 << 20
        ),
        cost_estimate=pl.CostEstimate(
            flops=4 * sections * cells * channels * hidden,
            bytes_accessed=4 * channels * hidden * 4,
            transcendentals=sections * cells * hidden,
        ),
        name="tower",
    )(feats, small, w_in, w_out, head_gain, head_proj)


def pair_terms(unit_rows, match_rows, yield_rows, first_global, logit_scale, logit_bias):
    logits = (
        logit_scale * jnp.dot(unit_rows, yield_rows.T, preferred_element_type=jnp.float32)
        + logit_bias
    )
    columns = first_global + jnp.arange(yield_rows.shape[0], dtype=jnp.int32)
    label = jnp.where(match_rows[:, None] == columns[None, :], 1.0, -1.0).astype(jnp.float32)
    coef = (-label * logit_scale * jax.nn.sigmoid(-label * logits)).astype(jnp.bfloat16)
    return jnp.dot(coef, yield_rows, preferred_element_type=jnp.float32)


def on_device(
    feats,
    dw_kernel,
    ln_gain,
    w_in,
    w_out,
    layer_scale,
    head_gain,
    head_proj,
    yield_embeds,
    match_ids,
    logit_scale,
    logit_bias,
):
    segment = lax.axis_index("pipe")
    taps = dw_kernel.shape[1]
    channels = feats.shape[-1]
    gathered = lax.all_gather(yield_embeds, "dp", axis=0, tiled=True)
    used = taps * taps + 2
    small = jnp.concatenate(
        [
            dw_kernel[0].reshape(taps * taps, channels).astype(jnp.float32),
            ln_gain,
            layer_scale,
            jnp.zeros((-used % 8, channels), jnp.float32),
        ],
        axis=0,
    )
    projected = tower(
        feats, small, w_in[0], w_out[0], head_gain[None, :], head_proj, taps
    ).reshape(feats.shape[0], -1)
    wide = projected.astype(jnp.float32)
    unit = (wide / jnp.sqrt(jnp.sum(wide * wide, axis=-1, keepdims=True) + 1e-06)).astype(
        jnp.bfloat16
    )
    row_base = segment * lax.axis_size("dp") * yield_embeds.shape[0]
    partial_grad = pair_terms(unit, match_ids, gathered, row_base, logit_scale, logit_bias)
    embed_grad = lax.psum(partial_grad.astype(jnp.bfloat16), "pipe").astype(jnp.float32)
    return (projected, embed_grad)


def solution(mesh):
    in_specs = (
        P("dp", None, None, None),
        P("pipe", None, None, None),
        P("pipe", None),
        P("pipe", None, None),
        P("pipe", None, None),
        P("pipe", None),
        P(),
        P(),
        P(("pipe", "dp"), None),
        P("dp"),
        P(),
        P(),
    )
    out_specs = (P("dp", None), P("dp", None))
    return jax.shard_map(
        on_device, mesh=mesh, in_specs=in_specs, out_specs=out_specs, check_vma=False
    )
```

```python
import functools

import jax
import jax.numpy as jnp
from jax import lax
from jax.experimental import pallas as pl
from jax.experimental.pallas import tpu as pltpu
from jax.sharding import PartitionSpec as P

CHUNK = 256
LANES = 128
ERF_POLY = (
    7.97872669e-01,
    3.63655561e-02,
    -5.77947342e-05,
    -4.72814832e-05,
    2.79985521e-06,
    -5.66473023e-08,
)
ERF_EDGE = 5.5 * 5.5


def gelu(x):
    x2 = jnp.minimum(x * x, ERF_EDGE)
    poly = ERF_POLY[-1]
    for coefficient in ERF_POLY[-2::-1]:
        poly = poly * x2 + coefficient
    half = 0.5 * x
    return half + half * jnp.tanh(x * poly)


def normalise(value, gain):
    mean = jnp.mean(value, axis=-1, keepdims=True)
    centred = value - mean
    var = jnp.mean(centred * centred, axis=-1, keepdims=True)
    return centred * lax.rsqrt(var + 1e-06) * gain


def tower_kernel(
    taps,
    grid,
    feats_hbm,
    small_hbm,
    win_hbm,
    wout_hbm,
    hgain_ref,
    hproj_ref,
    yields_hbm,
    match_ref,
    logit_scale_ref,
    logit_bias_ref,
    out_ref,
    grad_ref,
    feats,
    small,
    win,
    wout,
    act,
    conv,
    normed,
    acc,
    raw_a,
    raw_b,
    wide_taps,
    proj,
    pool_y,
    grads,
    feat_sem,
    small_sem,
    in_sem,
    out_sem,
    small_send,
    in_send,
    out_send,
    proj_send,
    proj_recv,
    grad_send,
    grad_recv,
    own_sem,
    z_send,
    z_recv,
    x_send,
    x_recv,
    y_send,
    y_recv,
):
    images, cols, rows, channels = feats.shape
    sections = win.shape[0]
    chunks = win.shape[1]
    places = rows * cols
    reach = taps // 2
    me = lax.axis_index("pipe")
    other = 1 - me
    peer = {"pipe": other}

    def in_source(c):
        return win_hbm.at[:, pl.ds(pl.multiple_of(c * CHUNK, CHUNK), CHUNK)]

    def out_source(c):
        return wout_hbm.at[pl.ds(pl.multiple_of(c * CHUNK, CHUNK), CHUNK), :]

    def local_small():
        return pltpu.make_async_copy(small_hbm, small.at[me], small_sem.at[me])

    def local_in(c):
        return pltpu.make_async_copy(in_source(c), win.at[me, c], in_sem.at[me, c])

    def local_out(c):
        return pltpu.make_async_copy(out_source(c), wout.at[me, c], out_sem.at[me, c])

    def remote(source, target, send, recv):
        return pltpu.make_async_remote_copy(
            src_ref=source,
            dst_ref=target,
            send_sem=send,
            recv_sem=recv,
            device_id=peer,
            device_id_type=pl.DeviceIdType.MESH,
        )

    def remote_small(section):
        return remote(small_hbm, small.at[section], small_send, small_sem.at[section])

    def remote_in(section, c):
        return remote(in_source(c), win.at[section, c], in_send.at[c], in_sem.at[section, c])

    def remote_out(section, c):
        return remote(out_source(c), wout.at[section, c], out_send.at[c], out_sem.at[section, c])

    deep, tall, wide = grid
    place = lax.axis_index("dp")
    at_z = place // (tall * wide)
    at_y = place // wide % tall
    at_x = place % wide

    def chip(z, y, x):
        return {"dp": (z * tall + y) * wide + x}

    def remote_to(source, target, send, recv, device):
        return pltpu.make_async_remote_copy(
            src_ref=source,
            dst_ref=target,
            send_sem=send,
            recv_sem=recv,
            device_id=device,
            device_id_type=pl.DeviceIdType.MESH,
        )

    def turn(value, step, count):
        return lax.rem(value + step, count)

    def z_copy(step):
        return remote_to(
            yields_hbm,
            pool_y.at[at_z, at_y, at_x],
            z_send.at[step],
            z_recv.at[step],
            chip(turn(at_z, step, deep), at_y, at_x),
        )

    def x_copy(step, half, second):
        part = pool_y.at[:, :, at_x, half] if second else pool_y.at[:, at_y, at_x, half]
        return remote_to(
            part,
            part,
            x_send.at[half, step],
            x_recv.at[half, step],
            chip(at_z, at_y, turn(at_x, step, wide)),
        )

    def y_copy(step, half, second):
        part = pool_y.at[:, at_y, :, half] if second else pool_y.at[:, at_y, at_x, half]
        return remote_to(
            part,
            part,
            y_send.at[half, step],
            y_recv.at[half, step],
            chip(at_z, turn(at_y, step, tall), at_x),
        )

    def x_arrival(step, half, second):
        source = turn(at_x, wide - step, wide)
        part = pool_y.at[:, :, source, half] if second else pool_y.at[:, at_y, source, half]
        return remote_to(
            part, part, x_send.at[half, step], x_recv.at[half, step], chip(at_z, at_y, source)
        )

    def y_arrival(step, half, second):
        source = turn(at_y, tall - step, tall)
        part = pool_y.at[:, source, :, half] if second else pool_y.at[:, source, at_x, half]
        return remote_to(
            part, part, y_send.at[half, step], y_recv.at[half, step], chip(at_z, source, at_x)
        )

    def z_arrival(step):
        source = turn(at_z, deep - step, deep)
        return remote_to(
            yields_hbm,
            pool_y.at[source, at_y, at_x],
            z_send.at[step],
            z_recv.at[step],
            chip(source, at_y, at_x),
        )

    own_yields = pltpu.make_async_copy(yields_hbm, pool_y.at[at_z, at_y, at_x], own_sem)

    def gather_begin():
        for step in range(1, deep):
            z_copy(step).start()
        own_yields.start()

    def gather_second():
        own_yields.wait()
        for step in range(1, deep):
            z_arrival(step).wait_recv()
        for step in range(1, wide):
            x_copy(step, 0, False).start()
        for step in range(1, tall):
            y_copy(step, 1, False).start()

    def gather_third():
        for step in range(1, wide):
            x_arrival(step, 0, False).wait_recv()
        for step in range(1, tall):
            y_arrival(step, 1, False).wait_recv()
        for step in range(1, tall):
            y_copy(step, 0, True).start()
        for step in range(1, wide):
            x_copy(step, 1, True).start()

    def gather_end():
        for step in range(1, tall):
            y_arrival(step, 0, True).wait_recv()
        for step in range(1, wide):
            x_arrival(step, 1, True).wait_recv()
        for step in range(1, deep):
            z_copy(step).wait_send()
        for step in range(1, wide):
            x_copy(step, 0, False).wait_send()
            x_copy(step, 1, True).wait_send()
        for step in range(1, tall):
            y_copy(step, 1, False).wait_send()
            y_copy(step, 0, True).wait_send()

    fetch = pltpu.make_async_copy(feats_hbm.at[pl.ds(me * images, images)], feats, feat_sem)
    fetch.start()
    local_small().start()

    barrier = pltpu.get_barrier_semaphore()
    pl.semaphore_signal(barrier, inc=1, device_id=peer, device_id_type=pl.DeviceIdType.MESH)
    neighbours = (
        [chip(turn(at_z, step, deep), at_y, at_x) for step in range(1, deep)]
        + [chip(at_z, turn(at_y, step, tall), at_x) for step in range(1, tall)]
        + [chip(at_z, at_y, turn(at_x, step, wide)) for step in range(1, wide)]
    )
    for neighbour in neighbours:
        pl.semaphore_signal(
            barrier, inc=1, device_id=neighbour, device_id_type=pl.DeviceIdType.MESH
        )
    pl.semaphore_wait(barrier, 1 + len(neighbours))

    remote_small(me).start()
    gather_begin()

    def begin(c, carry):
        remote_in(me, c).start()
        local_in(c).start()
        remote_out(me, c).start()
        local_out(c).start()
        return carry

    lax.fori_loop(0, chunks, begin, 0)

    def await_small(section):
        @pl.when(section == me)
        def _():
            local_small().wait()

        @pl.when(section != me)
        def _():
            remote_small(section).wait_recv()

    def await_chunk(section, c):
        @pl.when(section == me)
        def _():
            local_in(c).wait()
            local_out(c).wait()

        @pl.when(section != me)
        def _():
            remote_in(section, c).wait_recv()
            remote_out(section, c).wait_recv()

    fetch.wait()

    for image in range(images):
        for w in range(cols):
            line = feats[image, w].astype(jnp.float32)
            for block in range(channels // LANES):
                act[block, pl.ds(w * rows * images + image, rows, stride=images), :] = line[
                    :, block * LANES : (block + 1) * LANES
                ]

    def one_section(section, carry):
        await_small(section)

        def conv_lanes(block, inner):
            lanes = pl.ds(pl.multiple_of(block * LANES, LANES), LANES)
            for k in range(taps * taps):
                wide_taps[k] = jnp.broadcast_to(small[section, pl.ds(k, 1), lanes], (images, LANES))
            for r in range(rows):
                total = [None] * cols
                for dy in range(taps):
                    source = r + dy - reach
                    if not 0 <= source < rows:
                        continue
                    kernel = [wide_taps[dy * taps + dx] for dx in range(taps)]
                    line = [
                        act[block, pl.ds((w * rows + source) * images, images), :]
                        for w in range(cols)
                    ]
                    for w in range(cols):
                        for dx in range(taps):
                            at = w + dx - reach
                            if not 0 <= at < cols:
                                continue
                            term = line[at] * kernel[dx]
                            total[w] = term if total[w] is None else total[w] + term
                for w in range(cols):
                    conv[pl.ds((w * rows + r) * images, images), lanes] = total[w]
            return inner

        lax.fori_loop(0, channels // LANES, conv_lanes, 0)

        gain = small[section, pl.ds(taps * taps, 1), :]
        step_rows = 32

        def norm_rows(block, inner):
            at = pl.ds(pl.multiple_of(block * step_rows, step_rows), step_rows)
            normed[at, :] = normalise(conv[at, :], gain).astype(jnp.bfloat16)
            return inner

        lax.fori_loop(0, places * images // step_rows, norm_rows, 0, unroll=4)

        acc[...] = jnp.zeros_like(acc)
        await_chunk(section, 0)
        raw_a[...] = jnp.dot(normed[...], win[section, 0], preferred_element_type=jnp.float32)

        def pair(j, inner):
            first = 2 * j
            after = jnp.minimum(first + 2, chunks - 1)
            await_chunk(section, first + 1)

            @pl.when(jnp.logical_and(section == 0, j == chunks // 4))
            def _():
                gather_second()

            @pl.when(first + 2 < chunks)
            def _():
                await_chunk(section, after)

            raw_b[...] = jnp.dot(
                normed[...], win[section, first + 1], preferred_element_type=jnp.float32
            )
            acc[...] += jnp.dot(
                gelu(raw_a[...]).astype(jnp.bfloat16),
                wout[section, first],
                preferred_element_type=jnp.float32,
            )
            raw_a[...] = jnp.dot(
                normed[...], win[section, after], preferred_element_type=jnp.float32
            )
            acc[...] += jnp.dot(
                gelu(raw_b[...]).astype(jnp.bfloat16),
                wout[section, first + 1],
                preferred_element_type=jnp.float32,
            )
            return inner

        lax.fori_loop(0, chunks // 2, pair, 0)

        scale = small[section, pl.ds(taps * taps + 1, 1), :]

        def add_rows(block, inner):
            at = pl.ds(pl.multiple_of(block * step_rows, step_rows), step_rows)
            for lane in range(channels // LANES):
                lanes = slice(lane * LANES, (lane + 1) * LANES)
                total = act[lane, at, :] + scale[:, lanes] * acc[at, lanes]
                act[lane, at, :] = total.astype(jnp.bfloat16).astype(jnp.float32)
            return inner

        lax.fori_loop(0, places * images // step_rows, add_rows, 0, unroll=4)

        @pl.when(section == 0)
        def _():
            gather_third()

        return carry

    lax.fori_loop(0, sections, one_section, 0)

    def pool(place, total):
        at = pl.ds(pl.multiple_of(place * images, images), images)
        return tuple(part + act[lane, at, :] for lane, part in enumerate(total))

    start = (jnp.zeros((images, LANES), jnp.float32),) * (channels // LANES)
    pooled = lax.fori_loop(0, places, pool, start, unroll=8)
    pooled = jnp.concatenate(pooled, axis=1) * (1.0 / places)
    head = normalise(pooled, hgain_ref[...]).astype(jnp.bfloat16)
    proj[me] = jnp.dot(head, hproj_ref[...], preferred_element_type=jnp.float32).astype(
        jnp.bfloat16
    )
    swap = remote(proj.at[me], proj.at[me], proj_send, proj_recv)
    swap.start()

    gather_end()

    def finish(c, carry):
        remote_in(me, c).wait_send()
        remote_out(me, c).wait_send()
        return carry

    remote_small(me).wait_send()
    lax.fori_loop(0, chunks, finish, 0)
    swap.wait_send()
    remote(proj.at[other], proj.at[other], proj_send, proj_recv).wait_recv()
    out_ref[...] = proj[...]

    count = sections * images
    width = proj.shape[-1]
    projected = proj[...].astype(jnp.float32).reshape(count, width)
    length = jnp.sqrt(jnp.sum(projected * projected, axis=-1, keepdims=True) + 1e-06)
    unit = (projected / length).astype(jnp.bfloat16)
    logit_scale = logit_scale_ref[0]
    logit_bias = logit_bias_ref[0]
    match = match_ref[...]
    held = tall * wide * yields_hbm.shape[0] * yields_hbm.shape[1]

    def pairs(z, total):
        yields = pool_y[z].reshape(held, width)
        dots = lax.dot_general(
            unit, yields, (((1,), (1,)), ((), ())), preferred_element_type=jnp.float32
        )
        logits = logit_scale * dots + logit_bias
        first = (me * deep + z) * held
        columns = first + lax.broadcasted_iota(jnp.int32, (count, held), 1)
        label = jnp.where(match == columns, 1.0, -1.0)
        coef = (-label * logit_scale * jax.nn.sigmoid(-label * logits)).astype(jnp.bfloat16)
        return total + jnp.dot(coef, yields, preferred_element_type=jnp.float32)

    grads[me] = lax.fori_loop(
        0, deep, pairs, jnp.zeros((count, width), jnp.float32), unroll=min(deep, 4)
    )
    trade = remote(grads.at[me], grads.at[me], grad_send, grad_recv)
    trade.start()
    trade.wait_send()
    remote(grads.at[other], grads.at[other], grad_send, grad_recv).wait_recv()
    grad_ref[...] = grads[0] + grads[1]


def chip_grid(count):
    side = 1
    while 2 * side**3 < count:
        side += 1
    return (2 * side, side, side) if 2 * side**3 == count else (count, 1, 1)


def tower(feats, small, w_in, w_out, head_gain, head_proj, yields, match, scale, bias, taps):
    sections = lax.axis_size("pipe")
    images = feats.shape[0] // sections
    cols, rows, channels = feats.shape[1:]
    hidden = w_in.shape[1]
    width = head_proj.shape[1]
    chunks = hidden // CHUNK
    cells = rows * cols * images
    grid = chip_grid(lax.axis_size("dp"))
    f32, b16 = jnp.float32, jnp.bfloat16
    dma = pltpu.SemaphoreType.DMA
    anywhere = pl.BlockSpec(memory_space=pl.ANY)
    vmem = pl.BlockSpec(memory_space=pltpu.VMEM)
    smem = pl.BlockSpec(memory_space=pltpu.SMEM)
    return pl.pallas_call(
        functools.partial(tower_kernel, taps, grid),
        out_shape=(
            jax.ShapeDtypeStruct((sections, images, width), b16),
            jax.ShapeDtypeStruct((sections * images, width), f32),
        ),
        in_specs=[anywhere] * 4 + [vmem, vmem, anywhere, vmem, smem, smem],
        out_specs=(vmem, vmem),
        scratch_shapes=[
            pltpu.VMEM((images, cols, rows, channels), b16),
            pltpu.VMEM((sections,) + small.shape, f32),
            pltpu.VMEM((sections, chunks, channels, CHUNK), b16),
            pltpu.VMEM((sections, chunks, CHUNK, channels), b16),
            pltpu.VMEM((channels // LANES, cells, LANES), f32),
            pltpu.VMEM((cells, channels), f32),
            pltpu.VMEM((cells, channels), b16),
            pltpu.VMEM((cells, channels), f32),
            pltpu.VMEM((cells, CHUNK), f32),
            pltpu.VMEM((cells, CHUNK), f32),
            pltpu.VMEM((taps * taps, images, LANES), f32),
            pltpu.VMEM((sections, images, width), b16),
            pltpu.VMEM(grid + yields.shape, b16),
            pltpu.VMEM((sections, sections * images, width), f32),
            dma,
            dma((sections,)),
            dma((sections, chunks)),
            dma((sections, chunks)),
            dma,
            dma((chunks,)),
            dma((chunks,)),
            dma,
            dma,
            dma,
            dma,
            dma,
            dma((grid[0],)),
            dma((grid[0],)),
            dma((2, grid[2])),
            dma((2, grid[2])),
            dma((2, grid[1])),
            dma((2, grid[1])),
        ],
        compiler_params=pltpu.CompilerParams(
            collective_id=0, has_side_effects=True, vmem_limit_bytes=58 << 20
        ),
        cost_estimate=pl.CostEstimate(
            flops=4 * sections * cells * channels * hidden,
            bytes_accessed=4 * channels * hidden * 4,
            transcendentals=sections * cells * hidden,
        ),
        name="tower",
    )(feats, small, w_in, w_out, head_gain, head_proj, yields, match, scale, bias)


def on_device(
    feats,
    dw_kernel,
    ln_gain,
    w_in,
    w_out,
    layer_scale,
    head_gain,
    head_proj,
    yield_embeds,
    match_ids,
    logit_scale,
    logit_bias,
):
    taps = dw_kernel.shape[1]
    channels = feats.shape[-1]
    used = taps * taps + 2
    small = jnp.concatenate(
        [
            dw_kernel[0].reshape(taps * taps, channels).astype(jnp.float32),
            ln_gain,
            layer_scale,
            jnp.zeros((-used % 8, channels), jnp.float32),
        ],
        axis=0,
    )
    projected, embed_grad = tower(
        feats.transpose(0, 2, 1, 3),
        small,
        w_in[0],
        w_out[0],
        head_gain[None, :],
        head_proj,
        yield_embeds.reshape(2, yield_embeds.shape[0] // 2, yield_embeds.shape[1]),
        match_ids[:, None],
        logit_scale[None],
        logit_bias[None],
        taps,
    )
    return (projected.reshape(feats.shape[0], -1), embed_grad)


def solution(mesh):
    in_specs = (
        P("dp", None, None, None),
        P("pipe", None, None, None),
        P("pipe", None),
        P("pipe", None, None),
        P("pipe", None, None),
        P("pipe", None),
        P(),
        P(),
        P(("pipe", "dp"), None),
        P("dp"),
        P(),
        P(),
    )
    out_specs = (P("dp", None), P("dp", None))
    return jax.shard_map(
        on_device, mesh=mesh, in_specs=in_specs, out_specs=out_specs, check_vma=False
    )
```

```python
import functools

import jax
import jax.numpy as jnp
from jax import lax
from jax.experimental import pallas as pl
from jax.experimental.pallas import tpu as pltpu
from jax.sharding import PartitionSpec as P

CHUNK = 512
LANES = 128
ERF_POLY = (
    7.97872669e-01,
    3.63655561e-02,
    -5.77947342e-05,
    -4.72814832e-05,
    2.79985521e-06,
    -5.66473023e-08,
)
ERF_EDGE = 5.5 * 5.5


def gelu(x):
    x2 = jnp.minimum(x * x, ERF_EDGE)
    poly = ERF_POLY[-1]
    for coefficient in ERF_POLY[-2::-1]:
        poly = poly * x2 + coefficient
    half = 0.5 * x
    return half + half * jnp.tanh(x * poly)


def normalise(value, gain):
    mean = jnp.mean(value, axis=-1, keepdims=True)
    centred = value - mean
    var = jnp.mean(centred * centred, axis=-1, keepdims=True)
    return centred * lax.rsqrt(var + 1e-06) * gain


def tower_kernel(
    taps,
    grid,
    feats_hbm,
    small_hbm,
    win_hbm,
    wout_hbm,
    hgain_ref,
    hproj_ref,
    yields_hbm,
    match_ref,
    logit_scale_ref,
    logit_bias_ref,
    out_ref,
    grad_ref,
    feats,
    small,
    win,
    wout,
    act,
    conv,
    normed,
    acc,
    raw_a,
    raw_b,
    wide_taps,
    proj,
    pool_y,
    grads,
    feat_sem,
    small_sem,
    in_sem,
    out_sem,
    small_send,
    in_send,
    out_send,
    proj_send,
    proj_recv,
    grad_send,
    grad_recv,
    own_sem,
    z_send,
    z_recv,
    x_send,
    x_recv,
    y_send,
    y_recv,
):
    images, cols, rows, channels = feats.shape
    sections = win.shape[0]
    chunks = win.shape[1]
    places = rows * cols
    reach = taps // 2
    me = lax.axis_index("pipe")
    other = 1 - me
    peer = {"pipe": other}

    def in_source(c):
        return win_hbm.at[:, pl.ds(pl.multiple_of(c * CHUNK, CHUNK), CHUNK)]

    def out_source(c):
        return wout_hbm.at[pl.ds(pl.multiple_of(c * CHUNK, CHUNK), CHUNK), :]

    def local_small():
        return pltpu.make_async_copy(small_hbm, small.at[me], small_sem.at[me])

    def local_in(c):
        return pltpu.make_async_copy(in_source(c), win.at[me, c], in_sem.at[me, c])

    def local_out(c):
        return pltpu.make_async_copy(out_source(c), wout.at[me, c], out_sem.at[me, c])

    def remote(source, target, send, recv):
        return pltpu.make_async_remote_copy(
            src_ref=source,
            dst_ref=target,
            send_sem=send,
            recv_sem=recv,
            device_id=peer,
            device_id_type=pl.DeviceIdType.MESH,
        )

    def remote_small(section):
        return remote(small_hbm, small.at[section], small_send, small_sem.at[section])

    def remote_in(section, c):
        return remote(in_source(c), win.at[section, c], in_send.at[c], in_sem.at[section, c])

    def remote_out(section, c):
        return remote(out_source(c), wout.at[section, c], out_send.at[c], out_sem.at[section, c])

    deep, tall, wide = grid
    place = lax.axis_index("dp")
    at_z = place // (tall * wide)
    at_y = place // wide % tall
    at_x = place % wide

    def chip(z, y, x):
        return {"dp": (z * tall + y) * wide + x}

    def remote_to(source, target, send, recv, device):
        return pltpu.make_async_remote_copy(
            src_ref=source,
            dst_ref=target,
            send_sem=send,
            recv_sem=recv,
            device_id=device,
            device_id_type=pl.DeviceIdType.MESH,
        )

    def turn(value, step, count):
        return lax.rem(value + step, count)

    def z_copy(step):
        return remote_to(
            yields_hbm,
            pool_y.at[at_z, at_y, at_x],
            z_send.at[step],
            z_recv.at[step],
            chip(turn(at_z, step, deep), at_y, at_x),
        )

    def x_copy(step, half, second):
        part = pool_y.at[:, :, at_x, half] if second else pool_y.at[:, at_y, at_x, half]
        return remote_to(
            part,
            part,
            x_send.at[half, step],
            x_recv.at[half, step],
            chip(at_z, at_y, turn(at_x, step, wide)),
        )

    def y_copy(step, half, second):
        part = pool_y.at[:, at_y, :, half] if second else pool_y.at[:, at_y, at_x, half]
        return remote_to(
            part,
            part,
            y_send.at[half, step],
            y_recv.at[half, step],
            chip(at_z, turn(at_y, step, tall), at_x),
        )

    def x_arrival(step, half, second):
        source = turn(at_x, wide - step, wide)
        part = pool_y.at[:, :, source, half] if second else pool_y.at[:, at_y, source, half]
        return remote_to(
            part, part, x_send.at[half, step], x_recv.at[half, step], chip(at_z, at_y, source)
        )

    def y_arrival(step, half, second):
        source = turn(at_y, tall - step, tall)
        part = pool_y.at[:, source, :, half] if second else pool_y.at[:, source, at_x, half]
        return remote_to(
            part, part, y_send.at[half, step], y_recv.at[half, step], chip(at_z, source, at_x)
        )

    def z_arrival(step):
        source = turn(at_z, deep - step, deep)
        return remote_to(
            yields_hbm,
            pool_y.at[source, at_y, at_x],
            z_send.at[step],
            z_recv.at[step],
            chip(source, at_y, at_x),
        )

    own_yields = pltpu.make_async_copy(yields_hbm, pool_y.at[at_z, at_y, at_x], own_sem)

    def gather_begin():
        for step in range(1, deep):
            z_copy(step).start()
        own_yields.start()

    def gather_second():
        own_yields.wait()
        for step in range(1, deep):
            z_arrival(step).wait_recv()
        for step in range(1, wide):
            x_copy(step, 0, False).start()
        for step in range(1, tall):
            y_copy(step, 1, False).start()

    def gather_third():
        for step in range(1, wide):
            x_arrival(step, 0, False).wait_recv()
        for step in range(1, tall):
            y_arrival(step, 1, False).wait_recv()
        for step in range(1, tall):
            y_copy(step, 0, True).start()
        for step in range(1, wide):
            x_copy(step, 1, True).start()

    def gather_end():
        for step in range(1, tall):
            y_arrival(step, 0, True).wait_recv()
        for step in range(1, wide):
            x_arrival(step, 1, True).wait_recv()
        for step in range(1, deep):
            z_copy(step).wait_send()
        for step in range(1, wide):
            x_copy(step, 0, False).wait_send()
            x_copy(step, 1, True).wait_send()
        for step in range(1, tall):
            y_copy(step, 1, False).wait_send()
            y_copy(step, 0, True).wait_send()

    fetch = pltpu.make_async_copy(feats_hbm.at[pl.ds(me * images, images)], feats, feat_sem)
    fetch.start()
    local_small().start()

    barrier = pltpu.get_barrier_semaphore()
    pl.semaphore_signal(barrier, inc=1, device_id=peer, device_id_type=pl.DeviceIdType.MESH)
    neighbours = (
        [chip(turn(at_z, step, deep), at_y, at_x) for step in range(1, deep)]
        + [chip(at_z, turn(at_y, step, tall), at_x) for step in range(1, tall)]
        + [chip(at_z, at_y, turn(at_x, step, wide)) for step in range(1, wide)]
    )
    for neighbour in neighbours:
        pl.semaphore_signal(
            barrier, inc=1, device_id=neighbour, device_id_type=pl.DeviceIdType.MESH
        )
    pl.semaphore_wait(barrier, 1 + len(neighbours))

    remote_small(me).start()
    gather_begin()

    def begin(c, carry):
        remote_in(me, c).start()
        local_in(c).start()
        remote_out(me, c).start()
        local_out(c).start()
        return carry

    lax.fori_loop(0, chunks, begin, 0)

    def await_small(section):
        @pl.when(section == me)
        def _():
            local_small().wait()

        @pl.when(section != me)
        def _():
            remote_small(section).wait_recv()

    def await_chunk(section, c):
        @pl.when(section == me)
        def _():
            local_in(c).wait()
            local_out(c).wait()

        @pl.when(section != me)
        def _():
            remote_in(section, c).wait_recv()
            remote_out(section, c).wait_recv()

    fetch.wait()

    for image in range(images):
        for w in range(cols):
            line = feats[image, w].astype(jnp.float32)
            for block in range(channels // LANES):
                act[block, pl.ds(w * rows * images + image, rows, stride=images), :] = line[
                    :, block * LANES : (block + 1) * LANES
                ]

    def one_section(section, carry):
        await_small(section)

        def conv_lanes(block, inner):
            lanes = pl.ds(pl.multiple_of(block * LANES, LANES), LANES)
            for k in range(taps * taps):
                wide_taps[k] = jnp.broadcast_to(small[section, pl.ds(k, 1), lanes], (images, LANES))
            for r in range(rows):
                total = [None] * cols
                for dy in range(taps):
                    source = r + dy - reach
                    if not 0 <= source < rows:
                        continue
                    kernel = [wide_taps[dy * taps + dx] for dx in range(taps)]
                    line = [
                        act[block, pl.ds((w * rows + source) * images, images), :]
                        for w in range(cols)
                    ]
                    for w in range(cols):
                        for dx in range(taps):
                            at = w + dx - reach
                            if not 0 <= at < cols:
                                continue
                            term = line[at] * kernel[dx]
                            total[w] = term if total[w] is None else total[w] + term
                for w in range(cols):
                    conv[pl.ds((w * rows + r) * images, images), lanes] = total[w]
            return inner

        lax.fori_loop(0, channels // LANES, conv_lanes, 0)

        gain = small[section, pl.ds(taps * taps, 1), :]
        step_rows = 32

        def norm_rows(block, inner):
            at = pl.ds(pl.multiple_of(block * step_rows, step_rows), step_rows)
            normed[at, :] = normalise(conv[at, :], gain).astype(jnp.bfloat16)
            return inner

        lax.fori_loop(0, places * images // step_rows, norm_rows, 0, unroll=4)

        acc[...] = jnp.zeros_like(acc)
        await_chunk(section, 0)

        def enter(c):
            out = jnp.dot(normed[...], win[section, c], preferred_element_type=jnp.float32)
            return out.astype(raw_a.dtype)

        def leave(source, c):
            hidden = gelu(source[...]).astype(jnp.bfloat16)
            return jnp.dot(hidden, wout[section, c], preferred_element_type=jnp.float32)

        raw_a[...] = enter(0)

        def pair(j, more):
            first = 2 * j
            await_chunk(section, first + 1)

            @pl.when(jnp.logical_and(section == 0, j == chunks // 4))
            def _():
                gather_second()

            if more:
                await_chunk(section, first + 2)
            raw_b[...] = enter(first + 1)
            acc[...] += leave(raw_a, first)
            if more:
                raw_a[...] = enter(first + 2)
            acc[...] += leave(raw_b, first + 1)

        def pair_step(j, inner):
            pair(j, True)
            return inner

        lax.fori_loop(0, chunks // 2 - 1, pair_step, 0)
        pair(chunks // 2 - 1, False)

        scale = small[section, pl.ds(taps * taps + 1, 1), :]

        def add_rows(block, inner):
            at = pl.ds(pl.multiple_of(block * step_rows, step_rows), step_rows)
            for lane in range(channels // LANES):
                lanes = slice(lane * LANES, (lane + 1) * LANES)
                total = act[lane, at, :] + scale[:, lanes] * acc[at, lanes]
                act[lane, at, :] = total.astype(jnp.bfloat16).astype(jnp.float32)
            return inner

        lax.fori_loop(0, places * images // step_rows, add_rows, 0, unroll=4)

        @pl.when(section == 0)
        def _():
            gather_third()

        return carry

    lax.fori_loop(0, sections, one_section, 0)

    def pool(place, total):
        at = pl.ds(pl.multiple_of(place * images, images), images)
        return tuple(part + act[lane, at, :] for lane, part in enumerate(total))

    start = (jnp.zeros((images, LANES), jnp.float32),) * (channels // LANES)
    pooled = lax.fori_loop(0, places, pool, start, unroll=8)
    pooled = jnp.concatenate(pooled, axis=1) * (1.0 / places)
    head = normalise(pooled, hgain_ref[...]).astype(jnp.bfloat16)
    proj[me] = jnp.dot(head, hproj_ref[...], preferred_element_type=jnp.float32).astype(
        jnp.bfloat16
    )
    swap = remote(proj.at[me], proj.at[me], proj_send, proj_recv)
    swap.start()

    gather_end()

    def finish(c, carry):
        remote_in(me, c).wait_send()
        remote_out(me, c).wait_send()
        return carry

    remote_small(me).wait_send()
    lax.fori_loop(0, chunks, finish, 0)
    swap.wait_send()
    remote(proj.at[other], proj.at[other], proj_send, proj_recv).wait_recv()
    out_ref[...] = proj[...]

    count = sections * images
    width = proj.shape[-1]
    projected = proj[...].astype(jnp.float32).reshape(count, width)
    length = jnp.sqrt(jnp.sum(projected * projected, axis=-1, keepdims=True) + 1e-06)
    unit = (projected / length).astype(jnp.bfloat16)
    logit_scale = logit_scale_ref[0]
    logit_bias = logit_bias_ref[0]
    match = match_ref[...]
    held = tall * wide * yields_hbm.shape[0] * yields_hbm.shape[1]

    def pairs(z, total):
        yields = pool_y[z].reshape(held, width)
        dots = lax.dot_general(
            unit, yields, (((1,), (1,)), ((), ())), preferred_element_type=jnp.float32
        )
        logits = logit_scale * dots + logit_bias
        first = (me * deep + z) * held
        columns = first + lax.broadcasted_iota(jnp.int32, (count, held), 1)
        label = jnp.where(match == columns, 1.0, -1.0)
        coef = (-label * logit_scale * jax.nn.sigmoid(-label * logits)).astype(jnp.bfloat16)
        return total + jnp.dot(coef, yields, preferred_element_type=jnp.float32)

    grads[me] = lax.fori_loop(
        0, deep, pairs, jnp.zeros((count, width), jnp.float32), unroll=min(deep, 4)
    )
    trade = remote(grads.at[me], grads.at[me], grad_send, grad_recv)
    trade.start()
    trade.wait_send()
    remote(grads.at[other], grads.at[other], grad_send, grad_recv).wait_recv()
    grad_ref[...] = grads[0] + grads[1]


def chip_grid(count):
    side = 1
    while 2 * side**3 < count:
        side += 1
    return (2 * side, side, side) if 2 * side**3 == count else (count, 1, 1)


def tower(feats, small, w_in, w_out, head_gain, head_proj, yields, match, scale, bias, taps):
    sections = lax.axis_size("pipe")
    images = feats.shape[0] // sections
    cols, rows, channels = feats.shape[1:]
    hidden = w_in.shape[1]
    width = head_proj.shape[1]
    chunks = hidden // CHUNK
    cells = rows * cols * images
    grid = chip_grid(lax.axis_size("dp"))
    deep_bytes = 2 * lax.axis_size("dp") * yields.size
    f32, b16 = jnp.float32, jnp.bfloat16
    dma = pltpu.SemaphoreType.DMA
    anywhere = pl.BlockSpec(memory_space=pl.ANY)
    vmem = pl.BlockSpec(memory_space=pltpu.VMEM)
    smem = pl.BlockSpec(memory_space=pltpu.SMEM)
    return pl.pallas_call(
        functools.partial(tower_kernel, taps, grid),
        out_shape=(
            jax.ShapeDtypeStruct((sections, images, width), b16),
            jax.ShapeDtypeStruct((sections * images, width), f32),
        ),
        in_specs=[anywhere] * 4 + [vmem, vmem, anywhere, vmem, smem, smem],
        out_specs=(vmem, vmem),
        scratch_shapes=[
            pltpu.VMEM((images, cols, rows, channels), b16),
            pltpu.VMEM((sections,) + small.shape, f32),
            pltpu.VMEM((sections, chunks, channels, CHUNK), b16),
            pltpu.VMEM((sections, chunks, CHUNK, channels), b16),
            pltpu.VMEM((channels // LANES, cells, LANES), f32),
            pltpu.VMEM((cells, channels), f32),
            pltpu.VMEM((cells, channels), b16),
            pltpu.VMEM((cells, channels), f32),
            pltpu.VMEM((cells, CHUNK), b16),
            pltpu.VMEM((cells, CHUNK), b16),
            pltpu.VMEM((taps * taps, images, LANES), f32),
            pltpu.VMEM((sections, images, width), b16),
            pltpu.VMEM(grid + yields.shape, b16),
            pltpu.VMEM((sections, sections * images, width), f32),
            dma,
            dma((sections,)),
            dma((sections, chunks)),
            dma((sections, chunks)),
            dma,
            dma((chunks,)),
            dma((chunks,)),
            dma,
            dma,
            dma,
            dma,
            dma,
            dma((grid[0],)),
            dma((grid[0],)),
            dma((2, grid[2])),
            dma((2, grid[2])),
            dma((2, grid[1])),
            dma((2, grid[1])),
        ],
        compiler_params=pltpu.CompilerParams(
            collective_id=0, has_side_effects=True, vmem_limit_bytes=(36 << 20) + deep_bytes
        ),
        cost_estimate=pl.CostEstimate(
            flops=4 * sections * cells * channels * hidden,
            bytes_accessed=4 * channels * hidden * 4,
            transcendentals=sections * cells * hidden,
        ),
        name="tower",
    )(feats, small, w_in, w_out, head_gain, head_proj, yields, match, scale, bias)


def on_device(
    feats,
    dw_kernel,
    ln_gain,
    w_in,
    w_out,
    layer_scale,
    head_gain,
    head_proj,
    yield_embeds,
    match_ids,
    logit_scale,
    logit_bias,
):
    taps = dw_kernel.shape[1]
    channels = feats.shape[-1]
    used = taps * taps + 2
    small = jnp.concatenate(
        [
            dw_kernel[0].reshape(taps * taps, channels).astype(jnp.float32),
            ln_gain,
            layer_scale,
            jnp.zeros((-used % 8, channels), jnp.float32),
        ],
        axis=0,
    )
    projected, embed_grad = tower(
        feats.transpose(0, 2, 1, 3),
        small,
        w_in[0],
        w_out[0],
        head_gain[None, :],
        head_proj,
        yield_embeds.reshape(2, yield_embeds.shape[0] // 2, yield_embeds.shape[1]),
        match_ids[:, None],
        logit_scale[None],
        logit_bias[None],
        taps,
    )
    return (projected.reshape(feats.shape[0], -1), embed_grad)


def solution(mesh):
    in_specs = (
        P("dp", None, None, None),
        P("pipe", None, None, None),
        P("pipe", None),
        P("pipe", None, None),
        P("pipe", None, None),
        P("pipe", None),
        P(),
        P(),
        P(("pipe", "dp"), None),
        P("dp"),
        P(),
        P(),
    )
    out_specs = (P("dp", None), P("dp", None))
    return jax.shard_map(
        on_device, mesh=mesh, in_specs=in_specs, out_specs=out_specs, check_vma=False
    )
```
